32 devices in a mesh: tm: 8 (over z, x), slab: 4 (over y, core).
Axes of the slice: x: 2, y: 2, z: 4, core: 2. Of those that a mesh axis runs over, the one named last changes fastest.
Arguments:
- source: float32 [32, 256, 2048], P('tm', 'slab'), may hold values from -6 to 6
- guess: float32 [32, 256, 2048], P('tm', 'slab'), may hold values from -2.5 to 2.5
- field: float32 [32, 256, 2048], P('tm', 'slab'), may hold values from -2.5 to 2.5
Outputs:
- solution: float32 [32, 256, 2048], P('tm', 'slab')
- residual_new: float32 [32, 256, 2048], P('tm', 'slab')
- force: float32 [32, 256, 2048], P('tm', 'slab')
The draws below stay inside these ranges and needn't reach their ends.
All inputs are finite; a program needn't handle non-finite values.
Results may differ from the reference program's by a relative error of at most 0.000021.
Values sent between devices are 32-bit elements; how exact they have to be, the bound alone decides.
A program may use at most 64 MiB of HBM per device.

```python
import jax
import jax.numpy as jnp

COLS = 2048
NT = 32
NR = 256


def draw_source(key, part):
    ramp = (0.5 + jnp.arange(NT, dtype=jnp.float32) / (NT - 1))[:, None, None]
    base = jnp.clip(jax.random.normal(key, (NT, NR, COLS), jnp.float32), -4.0, 4.0)
    return base * ramp


def steps_of(own_key, shape, pieces, smallest, top_value):
    factor_of = 1.0
    for axis_at, parts in pieces:
        heights = jax.random.uniform(jax.random.fold_in(jax.random.fold_in(own_key, 6), axis_at), (parts,), jnp.float32, smallest / len(pieces), top_value / len(pieces))
        factor_of = factor_of * jnp.repeat(jnp.exp(heights), shape[axis_at] // parts).reshape((-1,) + (1,) * (len(shape) - 1 - axis_at))
    return factor_of


def noise(key, dims, width, reach, shards=(), kind=jnp.bfloat16):
    entries = width * jax.random.normal(key, dims, jnp.float32)
    if shards:
        entries = entries * steps_of(key, dims, shards, -0.22, 0.18)
    return jnp.clip(entries, -reach, reach).astype(kind)


def setup_inputs(seed: int = 0) -> dict:
    key_of = jax.random.split(jax.random.key(seed), 4)
    return {
        "source": draw_source(jax.random.fold_in(key_of[3], 71), 0),
        "guess": noise(key_of[1], (NT, NR, COLS), 0.3, 2.5, ((0, 8), (1, 4)), jnp.float32),
        "field": noise(key_of[2], (NT, NR, COLS), 0.3, 2.5, ((0, 8), (1, 4)), jnp.float32),
    }


HOP_WEIGHT = 0.125
BOSON_WEIGHT = 2.0


def hopping(padded, parity_even):
    center = padded[:, 1:-1, :]
    sideways = jnp.roll(center, 1, axis=2) + jnp.roll(center, -1, axis=2)
    vertical = jnp.where(parity_even, padded[:, 2:, :], padded[:, :-2, :])
    return center + HOP_WEIGHT * (sideways + vertical)


def reference(source, guess, field):
    slices_all, rows_all, columns_all = source.shape
    row_ids = jnp.arange(rows_all, dtype=jnp.int32)[:, None]
    column_ids = jnp.arange(columns_all, dtype=jnp.int32)[None, :]
    parity_even = ((row_ids + column_ids) % 2 == 0)[None]
    slice_ids = jnp.arange(slices_all, dtype=jnp.int32)
    sign_here = jnp.where(slice_ids == 0, -1.0, 1.0).astype(jnp.float32)[:, None, None]
    sign_after = jnp.where(slice_ids == slices_all - 1, -1.0, 1.0).astype(jnp.float32)[:, None, None]
    weights = jnp.exp(field)

    def kinetic(values):
        return hopping(jnp.pad(values, ((0, 0), (1, 1), (0, 0))), parity_even)

    def forward(values):
        hopped = kinetic(values)
        carried = weights * hopped
        image = values - sign_here * jnp.roll(carried, 1, axis=0)
        back = weights * sign_after * jnp.roll(image, -1, axis=0)
        return image, back, hopped

    def normal(values):
        image, back, hopped = forward(values)
        return image - kinetic(back)

    residual = source - normal(guess)
    norm_sq = jnp.sum(residual * residual)
    applied = normal(residual)
    curvature = jnp.sum(residual * applied)
    alpha = norm_sq / curvature
    solution = guess + alpha * residual
    residual_new = residual - alpha * applied
    image, back, hopped = forward(solution)
    force = BOSON_WEIGHT * field + 2.0 * back * hopped
    return solution, residual_new, force
```

```python
import functools

import jax
import jax.numpy as jnp
from jax import lax
from jax.experimental import pallas as pl
from jax.experimental.pallas import tpu as pltpu
from jax.sharding import PartitionSpec as P

HOP_WEIGHT = 0.125
BOSON_WEIGHT = 2.0
MESH = pl.DeviceIdType.MESH
TILE = 8
LANES = 128


def kernel(
    nt, ns, L, R, C,
    src_h, g_h, f_h, sol_o, rn_o, fo_o,
    gp, bp, rp, qp, f, q, hg, hr, im, w, car, carr, c0, gN, cin, cN, rin,
    acc, slabg, tmg,
    lsem, osem, hss, hrs, bss, brs, css, crs, s1s, s1r, s2s, s2r,
):
    NB = R // TILE
    last = L - 1
    tm, sl = lax.axis_index("tm"), lax.axis_index("slab")
    nxt_t, prv_t = lax.rem(tm + 1, nt), lax.rem(tm + nt - 1, nt)
    up_s, dn_s = lax.rem(sl + ns - 1, ns), lax.rem(sl + 1, ns)
    has_up, has_dn = sl > 0, sl < ns - 1
    s_b = jnp.where(tm == 0, -1.0, 1.0).astype(jnp.float32)
    s_n = jnp.where(tm == nt - 1, -1.0, 1.0).astype(jnp.float32)

    order = [last] + list(range(last))
    g_in = {t: pltpu.make_async_copy(g_h.at[t], gp.at[t, pl.ds(TILE, R)], lsem.at[0, t]) for t in order}
    f_in = {t: pltpu.make_async_copy(f_h.at[t], f.at[t], lsem.at[1, t]) for t in order}
    q_in = {t: pltpu.make_async_copy(src_h.at[t], q.at[t], lsem.at[2, t]) for t in order}
    for t in order:
        g_in[t].start()
        f_in[t].start()
    for t in range(L):
        q_in[t].start()

    barrier = pltpu.get_barrier_semaphore()
    for k in range(1, ns):
        pl.semaphore_signal(barrier, inc=1, device_id=(tm, lax.rem(sl + k, ns)), device_id_type=MESH)
    for k in range(1, nt):
        pl.semaphore_signal(barrier, inc=1, device_id=(lax.rem(tm + k, nt), sl), device_id_type=MESH)
    pl.semaphore_wait(barrier, ns - 1 + nt - 1)

    def to_prev(src, dst, k):
        return pltpu.make_async_remote_copy(
            src_ref=src, dst_ref=dst, send_sem=bss.at[k], recv_sem=brs.at[k],
            device_id=(prv_t, sl), device_id_type=MESH)

    def to_next(src, dst, send, recv):
        return pltpu.make_async_remote_copy(
            src_ref=src, dst_ref=dst, send_sem=send, recv_sem=recv,
            device_id=(nxt_t, sl), device_id_type=MESH)

    def halo(src, off, dst, lo, n, k):
        ts = pl.ds(lo, n)
        up = pltpu.make_async_remote_copy(
            src_ref=src.at[ts, pl.ds(off, TILE)], dst_ref=dst.at[ts, pl.ds(TILE + R, TILE)],
            send_sem=hss.at[k, 0], recv_sem=hrs.at[k, 0],
            device_id=(tm, up_s), device_id_type=MESH)
        dn = pltpu.make_async_remote_copy(
            src_ref=src.at[ts, pl.ds(off + R - TILE, TILE)], dst_ref=dst.at[ts, pl.ds(0, TILE)],
            send_sem=hss.at[k, 1], recv_sem=hrs.at[k, 1],
            device_id=(tm, dn_s), device_id_type=MESH)

        @pl.when(has_up)
        def _():
            up.start()

        @pl.when(has_dn)
        def _():
            dn.start()

        def wait():
            @pl.when(has_up)
            def _():
                up.wait_send()
                dn.wait_recv()

            @pl.when(has_dn)
            def _():
                dn.wait_send()
                up.wait_recv()

        return wait

    send_g = to_prev(g_h.at[0], gN, 0)
    send_g.start()
    x1 = halo(g_h, 0, gp, 0, L, 0)

    @pl.when(jnp.logical_not(has_up))
    def _():
        for p in (gp, bp, rp, qp):
            for t in range(L):
                p[t, 0:TILE, :] = jnp.zeros((TILE, C), jnp.float32)

    @pl.when(jnp.logical_not(has_dn))
    def _():
        for p in (gp, bp, rp, qp):
            for t in range(L):
                p[t, TILE + R:, :] = jnp.zeros((TILE, C), jnp.float32)

    sub = lax.broadcasted_iota(jnp.int32, (TILE, C), 0)
    col = lax.broadcasted_iota(jnp.int32, (TILE, C), 1)
    even = lax.rem(sub + col, 2) == 0

    def rows(i, pad=0):
        return pl.ds(pl.multiple_of(i * TILE + pad, TILE), TILE)

    def hop(p, t, i):
        cur = p[t, rows(i, TILE), :]
        below = pltpu.roll(jnp.where(sub == 0, p[t, rows(i, 2 * TILE), :], cur), TILE - 1, 0)
        above = pltpu.roll(jnp.where(sub == TILE - 1, p[t, rows(i), :], cur), 1, 0)
        side = pltpu.roll(cur, 1, 1) + pltpu.roll(cur, C - 1, 1)
        return cur, cur + HOP_WEIGHT * (side + jnp.where(even, below, above))

    def fold(x):
        x = x * x
        parts = [x[:, k * LANES:(k + 1) * LANES] for k in range(C // LANES)]
        while len(parts) > 1:
            odd = parts[len(parts) // 2 * 2:]
            parts = [a + b for a, b in zip(parts[::2], parts[1::2])] + odd
        return parts[0]

    def each(n, body, init=0):
        return lax.fori_loop(0, n * NB, lambda j, c: body(j // NB, j % NB, c), init)

    for t in order:
        g_in[t].wait()
        f_in[t].wait()
    x1()

    def body_a(_, i, c):
        cur, k = hop(gp, last, i)
        wv = jnp.exp(f[last, rows(i), :])
        w[last, rows(i), :] = wv
        hg[last, rows(i), :] = k
        car[rows(i), :] = wv * k
        return c

    each(1, body_a)
    send_car = to_next(car, cin, bss.at[1], brs.at[1])
    send_car.start()

    for t in range(L):
        q_in[t].wait()

    def body_b0(_, i, c):
        q[0, rows(i), :] = q[0, rows(i), :] - gp[0, rows(i, TILE), :]
        return c

    each(1, body_b0)

    def body_b(t, i, c):
        cur, k = hop(gp, t, i)
        wv = jnp.exp(f[t, rows(i), :])
        w[t, rows(i), :] = wv
        hg[t, rows(i), :] = k
        image = gp[t + 1, rows(i, TILE), :] - wv * k
        q[t + 1, rows(i), :] = q[t + 1, rows(i), :] - image
        bp[t, rows(i, TILE), :] = wv * image
        return c

    each(last, body_b)
    x2a = halo(bp, TILE, bp, 0, last, 1)
    x2a()

    def body_c(_, i, c):
        cur, k = hop(bp, 0, i)
        c0[rows(i), :] = q[0, rows(i), :] + k
        return c

    each(1, body_c)
    send_c = to_prev(c0, cN, 2)
    send_c.start()

    zero = jnp.zeros((TILE, LANES), jnp.float32)

    def body_r(base):
        def body(t, i, c):
            t = t + base
            cur, k = hop(bp, t, i)
            r = q[t, rows(i), :] + k
            rp[t, rows(i, TILE), :] = r
            return c + fold(r)
        return body

    norm = each(last - 1, body_r(1), zero)

    send_g.wait_recv()

    def body_d(_, i, c):
        image = s_n * gN[rows(i), :] - car[rows(i), :]
        bp[last, rows(i, TILE), :] = w[last, rows(i), :] * image
        return c

    each(1, body_d)
    x2b = halo(bp, TILE, bp, last, 1, 2)
    x2b()
    norm = each(1, body_r(last), norm)
    x3a = halo(rp, TILE, rp, 1, last, 3)
    x3a()

    def body_e(_, i, c):
        cur, k = hop(rp, last, i)
        hr[last, rows(i), :] = k
        carr[rows(i), :] = w[last, rows(i), :] * k
        return c

    each(1, body_e)
    send_r = [to_next(carr.at[pl.ds(i * TILE, TILE)], rin.at[pl.ds(i * TILE, TILE)], css.at[i], crs.at[i])
              for i in range(NB)]
    early = NB // 2
    for i in range(early):
        send_r[i].start()

    def body_f(base):
        def body(t, i, c):
            t = t + base
            cur, k = hop(rp, t, i)
            hr[t, rows(i), :] = k
            wv = w[t, rows(i), :]
            image = rp[t + 1, rows(i, TILE), :] - wv * k
            im[t + 1, rows(i), :] = image
            qp[t, rows(i, TILE), :] = wv * image
            return c + fold(image)
        return body

    curv = each(last - 1, body_f(1), zero)

    send_car.wait_recv()

    def body_g(_, i, c):
        r = c0[rows(i), :] + s_b * cin[rows(i), :]
        rp[0, rows(i, TILE), :] = r
        return c + fold(r)

    norm = each(1, body_g, norm)
    x3b = halo(rp, TILE, rp, 0, 1, 4)
    x3b()
    curv = each(1, body_f(0), curv)
    x4a = halo(qp, TILE, qp, 0, last, 5)
    x4a()

    def body_y(base):
        def body(t, i, c):
            t = t + base
            cur, k = hop(qp, t, i)
            im[t, rows(i), :] = im[t, rows(i), :] - k
            return c
        return body

    def body_y0(_, i, c):
        cur, k = hop(qp, 0, i)
        im[0, rows(i), :] = rp[0, rows(i, TILE), :] - k
        return c

    each(1, body_y0)
    each(last - 1, body_y(1))

    send_c.wait_recv()

    def body_h(_, i, c):
        carried = carr[rows(i), :]
        r_next = cN[rows(i), :] + s_n * car[rows(i), :]
        image = s_n * r_next - carried
        qp[last, rows(i, TILE), :] = w[last, rows(i), :] * image
        return c + fold(image)

    curv = each(1, body_h, curv)
    acc[0, 0] = norm
    acc[0, 1] = curv
    slabg[sl, 0] = norm
    slabg[sl, 1] = curv
    sum1 = []
    for k in range(1, ns):
        sum1.append(pltpu.make_async_remote_copy(
            src_ref=acc.at[0], dst_ref=slabg.at[sl], send_sem=s1s.at[k], recv_sem=s1r.at[k],
            device_id=(tm, lax.rem(sl + k, ns)), device_id_type=MESH))
        sum1[-1].start()
    x4b = halo(qp, TILE, qp, last, 1, 6)
    for k in range(1, ns):
        pltpu.make_async_remote_copy(
            src_ref=acc.at[0], dst_ref=slabg.at[lax.rem(sl + ns - k, ns)], send_sem=s1s.at[k], recv_sem=s1r.at[k],
            device_id=(tm, lax.rem(sl + k, ns)), device_id_type=MESH).wait_recv()
    total = slabg[0]
    for k in range(1, ns):
        total = total + slabg[k]
    acc[1] = total
    tmg[tm] = total
    sum2 = []
    for k in range(1, nt):
        sum2.append(pltpu.make_async_remote_copy(
            src_ref=acc.at[1], dst_ref=tmg.at[tm], send_sem=s2s.at[k], recv_sem=s2r.at[k],
            device_id=(lax.rem(tm + k, nt), sl), device_id_type=MESH))
        sum2[-1].start()
    for i in range(early, NB):
        send_r[i].start()
    x4b()
    each(1, body_y(last))
    for k in range(1, nt):
        pltpu.make_async_remote_copy(
            src_ref=acc.at[1], dst_ref=tmg.at[lax.rem(tm + nt - k, nt)], send_sem=s2s.at[k], recv_sem=s2r.at[k],
            device_id=(lax.rem(tm + k, nt), sl), device_id_type=MESH).wait_recv()
    total = tmg[0]
    for k in range(1, nt):
        total = total + tmg[k]
    alpha = (jnp.full((TILE, C), jnp.sum(total[0])) / jnp.full((TILE, C), jnp.sum(total[1])))

    def body_s(t, i, c):
        r = rp[t, rows(i, TILE), :]
        gp[t, rows(i, TILE), :] = gp[t, rows(i, TILE), :] + alpha * r
        back = bp[t, rows(i, TILE), :] + alpha * qp[t, rows(i, TILE), :]
        hopped = hg[t, rows(i), :] + alpha * hr[t, rows(i), :]
        f[t, rows(i), :] = BOSON_WEIGHT * f[t, rows(i), :] + 2.0 * (back * hopped)
        return c

    each(L, body_s)
    outs = []
    for t in range(L):
        outs.append(pltpu.make_async_copy(gp.at[t, pl.ds(TILE, R)], sol_o.at[t], osem.at[0, t]))
        outs.append(pltpu.make_async_copy(f.at[t], fo_o.at[t], osem.at[1, t]))
    for o in outs:
        o.start()

    def body_n(t, i, c):
        t = t + 1
        q[t, rows(i), :] = rp[t, rows(i, TILE), :] - alpha * im[t, rows(i), :]
        return c

    each(last, body_n)
    for t in range(1, L):
        outs.append(pltpu.make_async_copy(q.at[t], rn_o.at[t], osem.at[2, t]))
        outs[-1].start()
    for i in range(NB):
        send_r[i].wait_recv()
        d = pl.ds(i * TILE, TILE)
        q[0, d, :] = rp[0, pl.ds(TILE + i * TILE, TILE), :] - alpha * (im[0, d, :] - s_b * rin[d, :])
    outs.append(pltpu.make_async_copy(q.at[0], rn_o.at[0], osem.at[2, 0]))
    outs[-1].start()
    send_g.wait_send()
    send_car.wait_send()
    send_c.wait_send()
    for c in send_r + sum1 + sum2:
        c.wait_send()
    for o in outs:
        o.wait()


def on_device(source, guess, field):
    L, R, C = source.shape
    nt, ns = lax.axis_size("tm"), lax.axis_size("slab")
    NB = R // TILE
    f32 = jnp.float32
    padded = pltpu.VMEM((L, R + 2 * TILE, C), f32)
    whole = pltpu.VMEM((L, R, C), f32)
    one = pltpu.VMEM((R, C), f32)
    sems = lambda *shape: pltpu.SemaphoreType.DMA(shape)
    return pl.pallas_call(
        functools.partial(kernel, nt, ns, L, R, C),
        out_shape=[jax.ShapeDtypeStruct((L, R, C), f32)] * 3,
        in_specs=[pl.BlockSpec(memory_space=pl.ANY)] * 3,
        out_specs=[pl.BlockSpec(memory_space=pl.ANY)] * 3,
        scratch_shapes=[padded] * 4 + [whole] * 6 + [one] * 7 + [
            pltpu.VMEM((2, 2, TILE, LANES), f32),
            pltpu.VMEM((ns, 2, TILE, LANES), f32),
            pltpu.VMEM((nt, 2, TILE, LANES), f32),
            sems(3, L), sems(3, L), sems(7, 2), sems(7, 2), sems(3), sems(3),
            sems(NB), sems(NB), sems(ns), sems(ns), sems(nt), sems(nt),
        ],
        compiler_params=pltpu.CompilerParams(
            collective_id=0, has_side_effects=True, vmem_limit_bytes=48 * 1024 * 1024),
    )(source, guess, field)


def solution(mesh):
    specs = (P("tm", "slab", None),) * 3
    return jax.shard_map(on_device, mesh=mesh, in_specs=specs, out_specs=specs, check_vma=False)
```

```python
import functools

import jax
import jax.numpy as jnp
from jax import lax
from jax.experimental import pallas as pl
from jax.experimental.pallas import tpu as pltpu
from jax.sharding import PartitionSpec as P

HOP_WEIGHT = 0.125
BOSON_WEIGHT = 2.0
MESH = pl.DeviceIdType.MESH
TILE = 8
LANES = 128


def kernel(
    nt, ns, L, R, C,
    src_h, g_h, f_h, sol_o, rn_o, fo_o,
    gp, bp, rp, qp, f, q, hg, hr, im, w, car, carr, c0, gN, cin, cN, rin,
    acc, slabg, tmg,
    lsem, hss, hrs, bss, brs, css, crs, s1s, s1r, s2s, s2r,
):
    NB = R // TILE
    last = L - 1
    tm, sl = lax.axis_index("tm"), lax.axis_index("slab")
    nxt_t, prv_t = lax.rem(tm + 1, nt), lax.rem(tm + nt - 1, nt)
    up_s, dn_s = lax.rem(sl + ns - 1, ns), lax.rem(sl + 1, ns)
    has_up, has_dn = sl > 0, sl < ns - 1
    s_b = jnp.where(tm == 0, -1.0, 1.0).astype(jnp.float32)
    s_n = jnp.where(tm == nt - 1, -1.0, 1.0).astype(jnp.float32)

    order = [last] + list(range(last))
    g_in = {t: pltpu.make_async_copy(g_h.at[t], gp.at[t, pl.ds(TILE, R)], lsem.at[0, t]) for t in order}
    f_in = {t: pltpu.make_async_copy(f_h.at[t], f.at[t], lsem.at[1, t]) for t in order}
    q_in = {t: pltpu.make_async_copy(src_h.at[t], q.at[t], lsem.at[2, t]) for t in order}
    for t in order:
        g_in[t].start()
        f_in[t].start()
    for t in range(L):
        q_in[t].start()

    barrier = pltpu.get_barrier_semaphore()
    for k in range(1, ns):
        pl.semaphore_signal(barrier, inc=1, device_id=(tm, lax.rem(sl + k, ns)), device_id_type=MESH)
    for k in range(1, nt):
        pl.semaphore_signal(barrier, inc=1, device_id=(lax.rem(tm + k, nt), sl), device_id_type=MESH)
    pl.semaphore_wait(barrier, ns - 1 + nt - 1)

    def to_prev(src, dst, k):
        return pltpu.make_async_remote_copy(
            src_ref=src, dst_ref=dst, send_sem=bss.at[k], recv_sem=brs.at[k],
            device_id=(prv_t, sl), device_id_type=MESH)

    def to_next(src, dst, send, recv):
        return pltpu.make_async_remote_copy(
            src_ref=src, dst_ref=dst, send_sem=send, recv_sem=recv,
            device_id=(nxt_t, sl), device_id_type=MESH)

    def halo(src, off, dst, lo, n, k):
        ts = pl.ds(lo, n)
        up = pltpu.make_async_remote_copy(
            src_ref=src.at[ts, pl.ds(off, 1)], dst_ref=dst.at[ts, pl.ds(TILE + R, 1)],
            send_sem=hss.at[k, 0], recv_sem=hrs.at[k, 0],
            device_id=(tm, up_s), device_id_type=MESH)
        dn = pltpu.make_async_remote_copy(
            src_ref=src.at[ts, pl.ds(off + R - 1, 1)], dst_ref=dst.at[ts, pl.ds(TILE - 1, 1)],
            send_sem=hss.at[k, 1], recv_sem=hrs.at[k, 1],
            device_id=(tm, dn_s), device_id_type=MESH)

        @pl.when(has_up)
        def _():
            up.start()

        @pl.when(has_dn)
        def _():
            dn.start()

        def wait():
            @pl.when(has_up)
            def _():
                up.wait_send()
                dn.wait_recv()

            @pl.when(has_dn)
            def _():
                dn.wait_send()
                up.wait_recv()

        return wait

    send_g = to_prev(g_h.at[0], gN, 0)
    send_g.start()
    x1 = halo(g_h, 0, gp, 0, L, 0)

    @pl.when(jnp.logical_not(has_up))
    def _():
        for p in (gp, bp, rp, qp):
            for t in range(L):
                p[t, 0:TILE, :] = jnp.zeros((TILE, C), jnp.float32)

    @pl.when(jnp.logical_not(has_dn))
    def _():
        for p in (gp, bp, rp, qp):
            for t in range(L):
                p[t, TILE + R:, :] = jnp.zeros((TILE, C), jnp.float32)

    sub = lax.broadcasted_iota(jnp.int32, (TILE, C), 0)
    parity = lax.rem(
        lax.broadcasted_iota(jnp.int32, (TILE, LANES), 0) + lax.broadcasted_iota(jnp.int32, (TILE, LANES), 1), 2)
    even = jnp.concatenate([parity] * (C // LANES), axis=1) == 0

    def rows(i, pad=0):
        return pl.ds(pl.multiple_of(i * TILE + pad, TILE), TILE)

    def hop(p, t, i):
        cur = p[t, rows(i, TILE), :]
        below = pltpu.roll(jnp.where(sub == 0, p[t, rows(i, 2 * TILE), :], cur), TILE - 1, 0)
        above = pltpu.roll(jnp.where(sub == TILE - 1, p[t, rows(i), :], cur), 1, 0)
        side = pltpu.roll(cur, 1, 1) + pltpu.roll(cur, C - 1, 1)
        return cur, cur + HOP_WEIGHT * (side + jnp.where(even, below, above))

    def fold(x):
        x = x * x
        parts = [x[:, k * LANES:(k + 1) * LANES] for k in range(C // LANES)]
        while len(parts) > 1:
            odd = parts[len(parts) // 2 * 2:]
            parts = [a + b for a, b in zip(parts[::2], parts[1::2])] + odd
        return parts[0]

    def each(n, body, init=0):
        return lax.fori_loop(0, n * NB, lambda j, c: body(j // NB, j % NB, c), init)

    zero = jnp.zeros((TILE, LANES), jnp.float32)

    g_in[last].wait()
    f_in[last].wait()
    x1()

    def body_a(_, i, c):
        cur, k = hop(gp, last, i)
        wv = jnp.exp(f[last, rows(i), :])
        w[last, rows(i), :] = wv
        hg[last, rows(i), :] = k
        car[rows(i), :] = wv * k
        return c

    each(1, body_a)
    send_car = to_next(car, cin, bss.at[1], brs.at[1])
    send_car.start()

    for t in range(last):
        g_in[t].wait()
        f_in[t].wait()
    for t in range(L):
        q_in[t].wait()

    def body_b(base):
        def body(t, i, c):
            t = t + base
            cur, k = hop(gp, t, i)
            wv = jnp.exp(f[t, rows(i), :])
            w[t, rows(i), :] = wv
            hg[t, rows(i), :] = k
            image = gp[t + 1, rows(i, TILE), :] - wv * k
            q[t + 1, rows(i), :] = q[t + 1, rows(i), :] - image
            bp[t, rows(i, TILE), :] = wv * image
            return c
        return body

    each(1, body_b(0))
    x2c = halo(bp, TILE, bp, 0, 1, 7)
    each(last - 1, body_b(1))
    x2a = halo(bp, TILE, bp, 1, last - 1, 1)
    x2c()

    def body_c(_, i, c):
        cur, k = hop(bp, 0, i)
        c0[rows(i), :] = (q[0, rows(i), :] - gp[0, rows(i, TILE), :]) + k
        return c

    each(1, body_c)
    send_c = to_prev(c0, cN, 2)
    send_c.start()

    def body_r(base):
        def body(t, i, c):
            t = t + base
            cur, k = hop(bp, t, i)
            r = q[t, rows(i), :] + k
            rp[t, rows(i, TILE), :] = r
            return c + fold(r)
        return body

    x2a()
    send_g.wait_recv()

    def body_d(_, i, c):
        image = s_n * gN[rows(i), :] - car[rows(i), :]
        bp[last, rows(i, TILE), :] = w[last, rows(i), :] * image
        return c

    each(1, body_d)
    x2b = halo(bp, TILE, bp, last, 1, 2)
    norm = each(last - 1, body_r(1), zero)
    x3c = halo(rp, TILE, rp, 1, last - 1, 8)
    x2b()
    norm = each(1, body_r(last), norm)
    x3a = halo(rp, TILE, rp, last, 1, 3)
    x3c()
    x3a()

    def body_e(_, i, c):
        cur, k = hop(rp, last, i)
        hr[last, rows(i), :] = k
        carr[rows(i), :] = w[last, rows(i), :] * k
        return c

    each(1, body_e)
    send_r = [to_next(carr.at[pl.ds(i * TILE, TILE)], rin.at[pl.ds(i * TILE, TILE)], css.at[i], crs.at[i])
              for i in range(NB)]
    early = NB * 5 // 8
    for i in range(early):
        send_r[i].start()

    def body_f(base):
        def body(t, i, c):
            t = t + base
            cur, k = hop(rp, t, i)
            hr[t, rows(i), :] = k
            wv = w[t, rows(i), :]
            image = rp[t + 1, rows(i, TILE), :] - wv * k
            im[t + 1, rows(i), :] = image
            qp[t, rows(i, TILE), :] = wv * image
            return c + fold(image)
        return body

    send_car.wait_recv()

    def body_g(_, i, c):
        r = c0[rows(i), :] + s_b * cin[rows(i), :]
        rp[0, rows(i, TILE), :] = r
        return c + fold(r)

    norm = each(1, body_g, norm)
    x3b = halo(rp, TILE, rp, 0, 1, 4)
    curv = each(last - 1, body_f(1), zero)
    x3b()
    curv = each(1, body_f(0), curv)
    x4a = halo(qp, TILE, qp, 0, last, 5)

    def body_y(base):
        def body(t, i, c):
            t = t + base
            cur, k = hop(qp, t, i)
            im[t, rows(i), :] = im[t, rows(i), :] - k
            return c
        return body

    def body_y0(_, i, c):
        cur, k = hop(qp, 0, i)
        im[0, rows(i), :] = rp[0, rows(i, TILE), :] - k
        return c

    send_c.wait_recv()

    def body_h(_, i, c):
        carried = carr[rows(i), :]
        r_next = cN[rows(i), :] + s_n * car[rows(i), :]
        image = s_n * r_next - carried
        qp[last, rows(i, TILE), :] = w[last, rows(i), :] * image
        return c + fold(image)

    curv = each(1, body_h, curv)
    acc[0, 0] = norm
    acc[0, 1] = curv
    slabg[sl, 0] = norm
    slabg[sl, 1] = curv

    def gather(at, dst, axis, me, n, send, recv):
        def copy(k, slot):
            other = lax.rem(me + k, n)
            return pltpu.make_async_remote_copy(
                src_ref=acc.at[at], dst_ref=dst.at[slot], send_sem=send.at[k], recv_sem=recv.at[k],
                device_id=(other, sl) if axis == 0 else (tm, other), device_id_type=MESH)
        sent = [copy(k, me) for k in range(1, n)]
        for c in sent:
            c.start()

        def wait():
            for k in range(1, n):
                copy(k, lax.rem(me + n - k, n)).wait_recv()
            total = dst[0]
            for k in range(1, n):
                total = total + dst[k]
            return total
        return sent, wait

    sum1, wait1 = gather(0, slabg, 1, sl, ns, s1s, s1r)
    x4b = halo(qp, TILE, qp, last, 1, 6)
    total = wait1()
    acc[1] = total
    tmg[tm] = total
    sum2, wait2 = gather(1, tmg, 0, tm, nt, s2s, s2r)
    for i in range(early, NB):
        send_r[i].start()
    x4a()
    each(1, body_y0)
    each(last - 1, body_y(1))
    x4b()
    each(1, body_y(last))
    total = wait2()
    ratio = jnp.full((TILE, LANES), jnp.sum(total[0])) / jnp.full((TILE, LANES), jnp.sum(total[1]))
    alpha = jnp.concatenate([ratio] * (C // LANES), axis=1)

    def body_s(t, i, c):
        sol_o[t, rows(i), :] = gp[t, rows(i, TILE), :] + alpha * rp[t, rows(i, TILE), :]
        back = bp[t, rows(i, TILE), :] + alpha * qp[t, rows(i, TILE), :]
        hopped = hg[t, rows(i), :] + alpha * hr[t, rows(i), :]
        fo_o[t, rows(i), :] = BOSON_WEIGHT * f[t, rows(i), :] + 2.0 * (back * hopped)
        return c

    each(L, body_s)

    def body_n(t, i, c):
        t = t + 1
        rn_o[t, rows(i), :] = rp[t, rows(i, TILE), :] - alpha * im[t, rows(i), :]
        return c

    each(last, body_n)
    for i in range(NB):
        send_r[i].wait_recv()
        d = pl.ds(i * TILE, TILE)
        rn_o[0, d, :] = rp[0, pl.ds(TILE + i * TILE, TILE), :] - alpha * (im[0, d, :] - s_b * rin[d, :])
    send_g.wait_send()
    send_car.wait_send()
    send_c.wait_send()
    for c in send_r + sum1 + sum2:
        c.wait_send()


def write_out(L, a, b, c, x, y, z, sem):
    copies = [pltpu.make_async_copy(src.at[t], dst.at[t], sem.at[j, t])
              for j, (src, dst) in enumerate(((a, x), (b, y), (c, z))) for t in range(L)]
    for copy in copies:
        copy.start()
    for copy in copies:
        copy.wait()


def on_device(source, guess, field):
    L, R, C = source.shape
    nt, ns = lax.axis_size("tm"), lax.axis_size("slab")
    NB = R // TILE
    f32 = jnp.float32
    padded = pltpu.VMEM((L, R + 2 * TILE, C), f32)
    whole = pltpu.VMEM((L, R, C), f32)
    one = pltpu.VMEM((R, C), f32)
    sems = lambda *shape: pltpu.SemaphoreType.DMA(shape)
    outs = pl.pallas_call(
        functools.partial(kernel, nt, ns, L, R, C),
        out_shape=[jax.ShapeDtypeStruct((L, R, C), f32)] * 3,
        in_specs=[pl.BlockSpec(memory_space=pltpu.HBM)] * 3,
        out_specs=[pl.BlockSpec(memory_space=pltpu.VMEM)] * 3,
        scratch_shapes=[padded] * 4 + [whole] * 6 + [one] * 7 + [
            pltpu.VMEM((2, 2, TILE, LANES), f32),
            pltpu.VMEM((ns, 2, TILE, LANES), f32),
            pltpu.VMEM((nt, 2, TILE, LANES), f32),
            sems(3, L), sems(9, 2), sems(9, 2), sems(3), sems(3),
            sems(NB), sems(NB), sems(ns), sems(ns), sems(nt), sems(nt),
        ],
        compiler_params=pltpu.CompilerParams(
            collective_id=0, has_side_effects=True, vmem_limit_bytes=57 * 1024 * 1024),
    )(source, guess, field)
    return pl.pallas_call(
        functools.partial(write_out, L),
        out_shape=[jax.ShapeDtypeStruct((L, R, C), f32)] * 3,
        in_specs=[pl.BlockSpec(memory_space=pltpu.VMEM)] * 3,
        out_specs=[pl.BlockSpec(memory_space=pltpu.HBM)] * 3,
        scratch_shapes=[sems(3, L)],
        compiler_params=pltpu.CompilerParams(vmem_limit_bytes=8 * 1024 * 1024),
    )(*outs)


def solution(mesh):
    specs = (P("tm", "slab", None),) * 3
    return jax.shard_map(on_device, mesh=mesh, in_specs=specs, out_specs=specs, check_vma=False)
```

```python
import functools

import jax
import jax.numpy as jnp
from jax import lax
from jax.experimental import pallas as pl
from jax.experimental.pallas import tpu as pltpu
from jax.sharding import PartitionSpec as P

HOP_WEIGHT = 0.125
BOSON_WEIGHT = 2.0
MESH = pl.DeviceIdType.MESH
TILE = 8
LANES = 128


def kernel(
    nt, ns, L, R, C,
    src_h, g_h, f_h, sol_o, rn_o, fo_o,
    gp, bp, rp, qp, f, q, hg, hr, im, w, car, carr, c0, gN, cin, cN, rin,
    acc, slabg, tmg,
    lsem, hss, hrs, bss, brs, css, crs, s1s, s1r, s2s, s2r,
):
    NB = R // TILE
    last = L - 1
    tm, sl = lax.axis_index("tm"), lax.axis_index("slab")
    nxt_t, prv_t = lax.rem(tm + 1, nt), lax.rem(tm + nt - 1, nt)
    up_s, dn_s = lax.rem(sl + ns - 1, ns), lax.rem(sl + 1, ns)
    has_up, has_dn = sl > 0, sl < ns - 1
    s_b = jnp.where(tm == 0, -1.0, 1.0).astype(jnp.float32)
    s_n = jnp.where(tm == nt - 1, -1.0, 1.0).astype(jnp.float32)

    order = [last] + list(range(last))
    g_in = {t: pltpu.make_async_copy(g_h.at[t], gp.at[t, pl.ds(TILE, R)], lsem.at[0, t]) for t in order}
    f_in = {t: pltpu.make_async_copy(f_h.at[t], f.at[t], lsem.at[1, t]) for t in order}
    q_in = {t: pltpu.make_async_copy(src_h.at[t], q.at[t], lsem.at[2, t]) for t in order}
    for t in order:
        g_in[t].start()
        f_in[t].start()
    for t in range(L):
        q_in[t].start()

    barrier = pltpu.get_barrier_semaphore()
    for k in range(1, ns):
        pl.semaphore_signal(barrier, inc=1, device_id=(tm, lax.rem(sl + k, ns)), device_id_type=MESH)
    for k in range(1, nt):
        pl.semaphore_signal(barrier, inc=1, device_id=(lax.rem(tm + k, nt), sl), device_id_type=MESH)
    pl.semaphore_wait(barrier, ns - 1 + nt - 1)

    def to_prev(src, dst, k):
        return pltpu.make_async_remote_copy(
            src_ref=src, dst_ref=dst, send_sem=bss.at[k], recv_sem=brs.at[k],
            device_id=(prv_t, sl), device_id_type=MESH)

    def to_next(src, dst, send, recv):
        return pltpu.make_async_remote_copy(
            src_ref=src, dst_ref=dst, send_sem=send, recv_sem=recv,
            device_id=(nxt_t, sl), device_id_type=MESH)

    def halo(src, off, dst, lo, n, k):
        ts = pl.ds(lo, n)
        up = pltpu.make_async_remote_copy(
            src_ref=src.at[ts, pl.ds(off, 1)], dst_ref=dst.at[ts, pl.ds(TILE + R, 1)],
            send_sem=hss.at[k, 0], recv_sem=hrs.at[k, 0],
            device_id=(tm, up_s), device_id_type=MESH)
        dn = pltpu.make_async_remote_copy(
            src_ref=src.at[ts, pl.ds(off + R - 1, 1)], dst_ref=dst.at[ts, pl.ds(TILE - 1, 1)],
            send_sem=hss.at[k, 1], recv_sem=hrs.at[k, 1],
            device_id=(tm, dn_s), device_id_type=MESH)

        @pl.when(has_up)
        def _():
            up.start()

        @pl.when(has_dn)
        def _():
            dn.start()

        def wait():
            @pl.when(has_up)
            def _():
                up.wait_send()
                dn.wait_recv()

            @pl.when(has_dn)
            def _():
                dn.wait_send()
                up.wait_recv()

        return wait

    send_g = to_prev(g_h.at[0], gN, 0)
    send_g.start()
    x1 = halo(g_h, 0, gp, 0, L, 0)

    @pl.when(jnp.logical_not(has_up))
    def _():
        for p in (gp, bp, rp, qp):
            for t in range(L):
                p[t, 0:TILE, :] = jnp.zeros((TILE, C), jnp.float32)

    @pl.when(jnp.logical_not(has_dn))
    def _():
        for p in (gp, bp, rp, qp):
            for t in range(L):
                p[t, TILE + R:, :] = jnp.zeros((TILE, C), jnp.float32)

    sub = lax.broadcasted_iota(jnp.int32, (TILE, C), 0)
    parity = lax.rem(
        lax.broadcasted_iota(jnp.int32, (TILE, LANES), 0) + lax.broadcasted_iota(jnp.int32, (TILE, LANES), 1), 2)
    even = jnp.concatenate([parity] * (C // LANES), axis=1) == 0

    def rows(i, pad=0):
        return pl.ds(pl.multiple_of(i * TILE + pad, TILE), TILE)

    def hop(p, t, i):
        cur = p[t, rows(i, TILE), :]
        below = pltpu.roll(jnp.where(sub == 0, p[t, rows(i, 2 * TILE), :], cur), TILE - 1, 0)
        above = pltpu.roll(jnp.where(sub == TILE - 1, p[t, rows(i), :], cur), 1, 0)
        side = pltpu.roll(cur, 1, 1) + pltpu.roll(cur, C - 1, 1)
        return cur, cur + HOP_WEIGHT * (side + jnp.where(even, below, above))

    def fold(x):
        x = x * x
        parts = [x[:, k * LANES:(k + 1) * LANES] for k in range(C // LANES)]
        while len(parts) > 1:
            odd = parts[len(parts) // 2 * 2:]
            parts = [a + b for a, b in zip(parts[::2], parts[1::2])] + odd
        return parts[0]

    def each(n, body, init=0):
        return lax.fori_loop(0, n * NB, lambda j, c: body(j // NB, j % NB, c), init)

    zero = jnp.zeros((TILE, LANES), jnp.float32)

    g_in[last].wait()
    f_in[last].wait()
    x1()

    def body_a(_, i, c):
        cur, k = hop(gp, last, i)
        wv = jnp.exp(f[last, rows(i), :])
        w[last, rows(i), :] = wv
        hg[last, rows(i), :] = k
        car[rows(i), :] = wv * k
        return c

    each(1, body_a)
    send_car = to_next(car, cin, bss.at[1], brs.at[1])
    send_car.start()

    for t in range(last):
        g_in[t].wait()
        f_in[t].wait()
    for t in range(L):
        q_in[t].wait()

    def body_b(base):
        def body(t, i, c):
            t = t + base
            cur, k = hop(gp, t, i)
            wv = jnp.exp(f[t, rows(i), :])
            w[t, rows(i), :] = wv
            hg[t, rows(i), :] = k
            image = gp[t + 1, rows(i, TILE), :] - wv * k
            q[t + 1, rows(i), :] = q[t + 1, rows(i), :] - image
            bp[t, rows(i, TILE), :] = wv * image
            return c
        return body

    each(1, body_b(0))
    x2c = halo(bp, TILE, bp, 0, 1, 7)
    each(last - 1, body_b(1))
    x2a = halo(bp, TILE, bp, 1, last - 1, 1)
    x2c()

    def body_c(_, i, c):
        cur, k = hop(bp, 0, i)
        c0[rows(i), :] = (q[0, rows(i), :] - gp[0, rows(i, TILE), :]) + k
        return c

    each(1, body_c)
    send_c = to_prev(c0, cN, 2)

    def body_r(base):
        def body(t, i, c):
            t = t + base
            cur, k = hop(bp, t, i)
            r = q[t, rows(i), :] + k
            rp[t, rows(i, TILE), :] = r
            return c + fold(r)
        return body

    x2a()
    send_g.wait_recv()

    def body_d(_, i, c):
        image = s_n * gN[rows(i), :] - car[rows(i), :]
        bp[last, rows(i, TILE), :] = w[last, rows(i), :] * image
        return c

    each(1, body_d)
    x2b = halo(bp, TILE, bp, last, 1, 2)
    send_c.start()
    norm = each(last - 1, body_r(1), zero)
    x3c = halo(rp, TILE, rp, 1, last - 1, 8)
    x2b()
    norm = each(1, body_r(last), norm)
    x3a = halo(rp, TILE, rp, last, 1, 3)
    x3c()
    x3a()

    def body_e(_, i, c):
        cur, k = hop(rp, last, i)
        hr[last, rows(i), :] = k
        carr[rows(i), :] = w[last, rows(i), :] * k
        return c

    each(1, body_e)
    send_r = [to_next(carr.at[pl.ds(i * TILE, TILE)], rin.at[pl.ds(i * TILE, TILE)], css.at[i], crs.at[i])
              for i in range(NB)]
    early = NB * 4 // 8

    def body_f(base):
        def body(t, i, c):
            t = t + base
            cur, k = hop(rp, t, i)
            hr[t, rows(i), :] = k
            wv = w[t, rows(i), :]
            image = rp[t + 1, rows(i, TILE), :] - wv * k
            im[t + 1, rows(i), :] = image
            qp[t, rows(i, TILE), :] = wv * image
            return c + fold(image)
        return body

    send_car.wait_recv()

    def body_g(_, i, c):
        r = c0[rows(i), :] + s_b * cin[rows(i), :]
        rp[0, rows(i, TILE), :] = r
        return c + fold(r)

    norm = each(1, body_g, norm)
    x3b = halo(rp, TILE, rp, 0, 1, 4)
    curv = each(last - 1, body_f(1), zero)
    x3b()
    curv = each(1, body_f(0), curv)
    x4a = halo(qp, TILE, qp, 0, last, 5)

    def body_y(base):
        def body(t, i, c):
            t = t + base
            cur, k = hop(qp, t, i)
            im[t, rows(i), :] = im[t, rows(i), :] - k
            return c
        return body

    def body_y0(_, i, c):
        cur, k = hop(qp, 0, i)
        im[0, rows(i), :] = rp[0, rows(i, TILE), :] - k
        return c

    for i in range(early):
        send_r[i].start()
    send_c.wait_recv()

    def body_h(_, i, c):
        carried = carr[rows(i), :]
        r_next = cN[rows(i), :] + s_n * car[rows(i), :]
        image = s_n * r_next - carried
        qp[last, rows(i, TILE), :] = w[last, rows(i), :] * image
        return c + fold(image)

    curv = each(1, body_h, curv)
    acc[0, 0] = norm
    acc[0, 1] = curv
    slabg[sl, 0] = norm
    slabg[sl, 1] = curv

    def gather(at, dst, axis, me, n, send, recv):
        def copy(k, slot):
            other = lax.rem(me + k, n)
            return pltpu.make_async_remote_copy(
                src_ref=acc.at[at], dst_ref=dst.at[slot], send_sem=send.at[k], recv_sem=recv.at[k],
                device_id=(other, sl) if axis == 0 else (tm, other), device_id_type=MESH)
        sent = [copy(k, me) for k in range(1, n)]
        for c in sent:
            c.start()

        def wait():
            for k in range(1, n):
                copy(k, lax.rem(me + n - k, n)).wait_recv()
            total = dst[0]
            for k in range(1, n):
                total = total + dst[k]
            return total
        return sent, wait

    sum1, wait1 = gather(0, slabg, 1, sl, ns, s1s, s1r)
    x4b = halo(qp, TILE, qp, last, 1, 6)
    total = wait1()
    acc[1] = total
    tmg[tm] = total
    sum2, wait2 = gather(1, tmg, 0, tm, nt, s2s, s2r)
    for i in range(early, NB):
        send_r[i].start()
    x4a()
    each(1, body_y0)
    each(last - 1, body_y(1))
    x4b()
    each(1, body_y(last))
    total = wait2()
    ratio = jnp.full((TILE, LANES), jnp.sum(total[0])) / jnp.full((TILE, LANES), jnp.sum(total[1]))
    alpha = jnp.concatenate([ratio] * (C // LANES), axis=1)

    def body_s(t, i, c):
        sol_o[t, rows(i), :] = gp[t, rows(i, TILE), :] + alpha * rp[t, rows(i, TILE), :]
        back = bp[t, rows(i, TILE), :] + alpha * qp[t, rows(i, TILE), :]
        hopped = hg[t, rows(i), :] + alpha * hr[t, rows(i), :]
        fo_o[t, rows(i), :] = BOSON_WEIGHT * f[t, rows(i), :] + 2.0 * (back * hopped)
        return c

    each(L, body_s)

    def body_n(t, i, c):
        t = t + 1
        rn_o[t, rows(i), :] = rp[t, rows(i, TILE), :] - alpha * im[t, rows(i), :]
        return c

    each(last, body_n)
    for i in range(NB):
        send_r[i].wait_recv()
        d = pl.ds(i * TILE, TILE)
        rn_o[0, d, :] = rp[0, pl.ds(TILE + i * TILE, TILE), :] - alpha * (im[0, d, :] - s_b * rin[d, :])
    send_g.wait_send()
    send_car.wait_send()
    send_c.wait_send()
    for c in send_r + sum1 + sum2:
        c.wait_send()


def write_out(L, a, b, c, x, y, z, sem):
    copies = [pltpu.make_async_copy(src.at[t], dst.at[t], sem.at[j, t])
              for j, (src, dst) in enumerate(((a, x), (b, y), (c, z))) for t in range(L)]
    for copy in copies:
        copy.start()
    for copy in copies:
        copy.wait()


def on_device(source, guess, field):
    L, R, C = source.shape
    nt, ns = lax.axis_size("tm"), lax.axis_size("slab")
    NB = R // TILE
    f32 = jnp.float32
    padded = pltpu.VMEM((L, R + 2 * TILE, C), f32)
    whole = pltpu.VMEM((L, R, C), f32)
    one = pltpu.VMEM((R, C), f32)
    sems = lambda *shape: pltpu.SemaphoreType.DMA(shape)
    outs = pl.pallas_call(
        functools.partial(kernel, nt, ns, L, R, C),
        out_shape=[jax.ShapeDtypeStruct((L, R, C), f32)] * 3,
        in_specs=[pl.BlockSpec(memory_space=pltpu.HBM)] * 3,
        out_specs=[pl.BlockSpec(memory_space=pltpu.VMEM)] * 3,
        scratch_shapes=[padded] * 4 + [whole] * 6 + [one] * 7 + [
            pltpu.VMEM((2, 2, TILE, LANES), f32),
            pltpu.VMEM((ns, 2, TILE, LANES), f32),
            pltpu.VMEM((nt, 2, TILE, LANES), f32),
            sems(3, L), sems(9, 2), sems(9, 2), sems(3), sems(3),
            sems(NB), sems(NB), sems(ns), sems(ns), sems(nt), sems(nt),
        ],
        compiler_params=pltpu.CompilerParams(
            collective_id=0, has_side_effects=True, vmem_limit_bytes=40 * 1024 * 1024),
    )(*(pltpu.with_memory_space_constraint(x, pltpu.HBM) for x in (source, guess, field)))
    return pl.pallas_call(
        functools.partial(write_out, L),
        out_shape=[jax.ShapeDtypeStruct((L, R, C), f32)] * 3,
        in_specs=[pl.BlockSpec(memory_space=pltpu.VMEM)] * 3,
        out_specs=[pl.BlockSpec(memory_space=pltpu.HBM)] * 3,
        scratch_shapes=[sems(3, L)],
        compiler_params=pltpu.CompilerParams(vmem_limit_bytes=8 * 1024 * 1024),
    )(*outs)


def solution(mesh):
    specs = (P("tm", "slab", None),) * 3
    return jax.shard_map(on_device, mesh=mesh, in_specs=specs, out_specs=specs, check_vma=False)
```

```python
import functools

import jax
import jax.numpy as jnp
from jax import lax
from jax.experimental import pallas as pl
from jax.experimental.pallas import tpu as pltpu
from jax.sharding import PartitionSpec as P

HOP_WEIGHT = 0.125
BOSON_WEIGHT = 2.0
MESH = pl.DeviceIdType.MESH
TILE = 8
LANES = 128


def kernel(
    nt, ns, L, R, C,
    src_h, g_h, f_h, sol_o, rn_o, fo_o,
    gp, bp, rp, qp, f, q, hg, hr, im, w, car, carr, c0, gN, cin, cN, rin,
    acc, slabg, tmg,
    lsem, hss, hrs, bss, brs, css, crs, s1s, s1r, s2s, s2r,
):
    NB = R // TILE
    last = L - 1
    tm, sl = lax.axis_index("tm"), lax.axis_index("slab")
    nxt_t, prv_t = lax.rem(tm + 1, nt), lax.rem(tm + nt - 1, nt)
    up_s, dn_s = lax.rem(sl + ns - 1, ns), lax.rem(sl + 1, ns)
    has_up, has_dn = sl > 0, sl < ns - 1
    s_b = jnp.where(tm == 0, -1.0, 1.0).astype(jnp.float32)
    s_n = jnp.where(tm == nt - 1, -1.0, 1.0).astype(jnp.float32)

    order = [last] + list(range(last))
    g_in = {t: pltpu.make_async_copy(g_h.at[t], gp.at[t, pl.ds(TILE, R)], lsem.at[0, t]) for t in order}
    f_in = {t: pltpu.make_async_copy(f_h.at[t], f.at[t], lsem.at[1, t]) for t in order}
    q_in = {t: pltpu.make_async_copy(src_h.at[t], q.at[t], lsem.at[2, t]) for t in order}
    for t in order:
        g_in[t].start()
        f_in[t].start()
    for t in range(L):
        q_in[t].start()

    barrier = pltpu.get_barrier_semaphore()
    for k in range(1, ns):
        pl.semaphore_signal(barrier, inc=1, device_id=(tm, lax.rem(sl + k, ns)), device_id_type=MESH)
    for k in range(1, nt):
        pl.semaphore_signal(barrier, inc=1, device_id=(lax.rem(tm + k, nt), sl), device_id_type=MESH)
    pl.semaphore_wait(barrier, ns - 1 + nt - 1)

    def to_prev(src, dst, k):
        return pltpu.make_async_remote_copy(
            src_ref=src, dst_ref=dst, send_sem=bss.at[k], recv_sem=brs.at[k],
            device_id=(prv_t, sl), device_id_type=MESH)

    def to_next(src, dst, send, recv):
        return pltpu.make_async_remote_copy(
            src_ref=src, dst_ref=dst, send_sem=send, recv_sem=recv,
            device_id=(nxt_t, sl), device_id_type=MESH)

    def halo(src, off, dst, lo, n, k):
        ts = pl.ds(lo, n)
        up = pltpu.make_async_remote_copy(
            src_ref=src.at[ts, pl.ds(off, 1)], dst_ref=dst.at[ts, pl.ds(TILE + R, 1)],
            send_sem=hss.at[k, 0], recv_sem=hrs.at[k, 0],
            device_id=(tm, up_s), device_id_type=MESH)
        dn = pltpu.make_async_remote_copy(
            src_ref=src.at[ts, pl.ds(off + R - 1, 1)], dst_ref=dst.at[ts, pl.ds(TILE - 1, 1)],
            send_sem=hss.at[k, 1], recv_sem=hrs.at[k, 1],
            device_id=(tm, dn_s), device_id_type=MESH)

        @pl.when(has_up)
        def _():
            up.start()

        @pl.when(has_dn)
        def _():
            dn.start()

        def wait():
            @pl.when(has_up)
            def _():
                up.wait_send()
                dn.wait_recv()

            @pl.when(has_dn)
            def _():
                dn.wait_send()
                up.wait_recv()

        return wait

    send_g = to_prev(g_h.at[0], gN, 0)
    send_g.start()
    x1 = halo(g_h, 0, gp, 0, L, 0)

    @pl.when(jnp.logical_not(has_up))
    def _():
        for p in (gp, bp, rp, qp):
            for t in range(L):
                p[t, 0:TILE, :] = jnp.zeros((TILE, C), jnp.float32)

    @pl.when(jnp.logical_not(has_dn))
    def _():
        for p in (gp, bp, rp, qp):
            for t in range(L):
                p[t, TILE + R:, :] = jnp.zeros((TILE, C), jnp.float32)

    sub = lax.broadcasted_iota(jnp.int32, (TILE, C), 0)
    parity = lax.rem(
        lax.broadcasted_iota(jnp.int32, (TILE, LANES), 0) + lax.broadcasted_iota(jnp.int32, (TILE, LANES), 1), 2)
    even = jnp.concatenate([parity] * (C // LANES), axis=1) == 0

    def rows(i, pad=0):
        return pl.ds(pl.multiple_of(i * TILE + pad, TILE), TILE)

    def hop(p, t, i):
        cur = p[t, rows(i, TILE), :]
        below = pltpu.roll(jnp.where(sub == 0, p[t, rows(i, 2 * TILE), :], cur), TILE - 1, 0)
        above = pltpu.roll(jnp.where(sub == TILE - 1, p[t, rows(i), :], cur), 1, 0)
        side = pltpu.roll(cur, 1, 1) + pltpu.roll(cur, C - 1, 1)
        return cur, cur + HOP_WEIGHT * (side + jnp.where(even, below, above))

    def fold(x):
        x = x * x
        parts = [x[:, k * LANES:(k + 1) * LANES] for k in range(C // LANES)]
        while len(parts) > 1:
            odd = parts[len(parts) // 2 * 2:]
            parts = [a + b for a, b in zip(parts[::2], parts[1::2])] + odd
        return parts[0]

    def each(n, body, init=0):
        return lax.fori_loop(0, n * NB, lambda j, c: body(j // NB, j % NB, c), init)

    zero = jnp.zeros((TILE, LANES), jnp.float32)

    g_in[last].wait()
    f_in[last].wait()
    x1()

    def body_a(_, i, c):
        cur, k = hop(gp, last, i)
        wv = jnp.exp(f[last, rows(i), :])
        w[last, rows(i), :] = wv
        hg[last, rows(i), :] = k
        car[rows(i), :] = wv * k
        return c

    each(1, body_a)
    send_car = to_next(car, cin, bss.at[1], brs.at[1])
    send_car.start()

    for t in range(last):
        g_in[t].wait()
        f_in[t].wait()
    for t in range(L):
        q_in[t].wait()

    def body_b(base):
        def body(t, i, c):
            t = t + base
            cur, k = hop(gp, t, i)
            wv = jnp.exp(f[t, rows(i), :])
            w[t, rows(i), :] = wv
            hg[t, rows(i), :] = k
            image = gp[t + 1, rows(i, TILE), :] - wv * k
            q[t + 1, rows(i), :] = q[t + 1, rows(i), :] - image
            bp[t, rows(i, TILE), :] = wv * image
            return c
        return body

    each(1, body_b(0))
    x2c = halo(bp, TILE, bp, 0, 1, 7)
    each(last - 1, body_b(1))
    x2a = halo(bp, TILE, bp, 1, last - 1, 1)
    x2c()

    def body_c(_, i, c):
        cur, k = hop(bp, 0, i)
        c0[rows(i), :] = (q[0, rows(i), :] - gp[0, rows(i, TILE), :]) + k
        return c

    each(1, body_c)
    send_c = to_prev(c0, cN, 2)

    def body_r(base):
        def body(t, i, c):
            t = t + base
            cur, k = hop(bp, t, i)
            r = q[t, rows(i), :] + k
            rp[t, rows(i, TILE), :] = r
            return c + fold(r)
        return body

    x2a()
    send_g.wait_recv()

    def body_d(_, i, c):
        image = s_n * gN[rows(i), :] - car[rows(i), :]
        bp[last, rows(i, TILE), :] = w[last, rows(i), :] * image
        return c

    each(1, body_d)
    x2b = halo(bp, TILE, bp, last, 1, 2)
    send_c.start()
    norm = each(last - 1, body_r(1), zero)
    x3c = halo(rp, TILE, rp, 1, last - 1, 8)
    x2b()
    norm = each(1, body_r(last), norm)
    x3a = halo(rp, TILE, rp, last, 1, 3)
    x3c()
    x3a()

    def body_e(_, i, c):
        cur, k = hop(rp, last, i)
        hr[last, rows(i), :] = k
        carr[rows(i), :] = w[last, rows(i), :] * k
        return c

    each(1, body_e)
    send_r = [to_next(carr.at[pl.ds(i * TILE, TILE)], rin.at[pl.ds(i * TILE, TILE)], css.at[i], crs.at[i])
              for i in range(NB)]
    early, mid = NB * 2 // 8, NB * 5 // 8

    def body_f(base):
        def body(t, i, c):
            t = t + base
            cur, k = hop(rp, t, i)
            hr[t, rows(i), :] = k
            wv = w[t, rows(i), :]
            image = rp[t + 1, rows(i, TILE), :] - wv * k
            im[t + 1, rows(i), :] = image
            qp[t, rows(i, TILE), :] = wv * image
            return c + fold(image)
        return body

    send_car.wait_recv()

    def body_g(_, i, c):
        r = c0[rows(i), :] + s_b * cin[rows(i), :]
        rp[0, rows(i, TILE), :] = r
        return c + fold(r)

    norm = each(1, body_g, norm)
    x3b = halo(rp, TILE, rp, 0, 1, 4)
    curv = each(last - 1, body_f(1), zero)
    x3b()
    curv = each(1, body_f(0), curv)
    x4a = halo(qp, TILE, qp, 0, last, 5)

    def body_y(base):
        def body(t, i, c):
            t = t + base
            cur, k = hop(qp, t, i)
            im[t, rows(i), :] = im[t, rows(i), :] - k
            return c
        return body

    def body_y0(_, i, c):
        cur, k = hop(qp, 0, i)
        im[0, rows(i), :] = rp[0, rows(i, TILE), :] - k
        return c

    for i in range(early):
        send_r[i].start()
    send_c.wait_recv()
    for i in range(early, mid):
        send_r[i].start()

    def body_h(_, i, c):
        carried = carr[rows(i), :]
        r_next = cN[rows(i), :] + s_n * car[rows(i), :]
        image = s_n * r_next - carried
        qp[last, rows(i, TILE), :] = w[last, rows(i), :] * image
        return c + fold(image)

    curv = each(1, body_h, curv)
    acc[0, 0] = norm
    acc[0, 1] = curv
    slabg[sl, 0] = norm
    slabg[sl, 1] = curv

    def gather(at, dst, axis, me, n, send, recv):
        def copy(k, slot):
            other = lax.rem(me + k, n)
            return pltpu.make_async_remote_copy(
                src_ref=acc.at[at], dst_ref=dst.at[slot], send_sem=send.at[k], recv_sem=recv.at[k],
                device_id=(other, sl) if axis == 0 else (tm, other), device_id_type=MESH)
        sent = [copy(k, me) for k in range(1, n)]
        for c in sent:
            c.start()

        def wait():
            for k in range(1, n):
                copy(k, lax.rem(me + n - k, n)).wait_recv()
            total = dst[0]
            for k in range(1, n):
                total = total + dst[k]
            return total
        return sent, wait

    sum1, wait1 = gather(0, slabg, 1, sl, ns, s1s, s1r)
    x4b = halo(qp, TILE, qp, last, 1, 6)
    total = wait1()
    acc[1] = total
    tmg[tm] = total
    sum2, wait2 = gather(1, tmg, 0, tm, nt, s2s, s2r)
    for i in range(mid, NB):
        send_r[i].start()
    x4a()
    each(1, body_y0)
    each(last - 1, body_y(1))
    x4b()
    each(1, body_y(last))
    total = wait2()
    ratio = jnp.full((TILE, LANES), jnp.sum(total[0])) / jnp.full((TILE, LANES), jnp.sum(total[1]))
    alpha = jnp.concatenate([ratio] * (C // LANES), axis=1)

    def body_s(t, i, c):
        sol_o[t, rows(i), :] = gp[t, rows(i, TILE), :] + alpha * rp[t, rows(i, TILE), :]
        back = bp[t, rows(i, TILE), :] + alpha * qp[t, rows(i, TILE), :]
        hopped = hg[t, rows(i), :] + alpha * hr[t, rows(i), :]
        fo_o[t, rows(i), :] = BOSON_WEIGHT * f[t, rows(i), :] + 2.0 * (back * hopped)
        return c

    each(L, body_s)

    def body_n(t, i, c):
        t = t + 1
        rn_o[t, rows(i), :] = rp[t, rows(i, TILE), :] - alpha * im[t, rows(i), :]
        return c

    each(last, body_n)
    for i in range(NB):
        send_r[i].wait_recv()
        d = pl.ds(i * TILE, TILE)
        rn_o[0, d, :] = rp[0, pl.ds(TILE + i * TILE, TILE), :] - alpha * (im[0, d, :] - s_b * rin[d, :])
    send_g.wait_send()
    send_car.wait_send()
    send_c.wait_send()
    for c in send_r + sum1 + sum2:
        c.wait_send()


def write_out(L, a, b, c, x, y, z, sem):
    copies = [pltpu.make_async_copy(src.at[t], dst.at[t], sem.at[j, t])
              for j, (src, dst) in enumerate(((a, x), (b, y), (c, z))) for t in range(L)]
    for copy in copies:
        copy.start()
    for copy in copies:
        copy.wait()


def on_device(source, guess, field):
    L, R, C = source.shape
    nt, ns = lax.axis_size("tm"), lax.axis_size("slab")
    NB = R // TILE
    f32 = jnp.float32
    padded = pltpu.VMEM((L, R + 2 * TILE, C), f32)
    whole = pltpu.VMEM((L, R, C), f32)
    one = pltpu.VMEM((R, C), f32)
    sems = lambda *shape: pltpu.SemaphoreType.DMA(shape)
    outs = pl.pallas_call(
        functools.partial(kernel, nt, ns, L, R, C),
        out_shape=[jax.ShapeDtypeStruct((L, R, C), f32)] * 3,
        in_specs=[pl.BlockSpec(memory_space=pltpu.HBM)] * 3,
        out_specs=[pl.BlockSpec(memory_space=pltpu.VMEM)] * 3,
        scratch_shapes=[padded] * 4 + [whole] * 6 + [one] * 7 + [
            pltpu.VMEM((2, 2, TILE, LANES), f32),
            pltpu.VMEM((ns, 2, TILE, LANES), f32),
            pltpu.VMEM((nt, 2, TILE, LANES), f32),
            sems(3, L), sems(9, 2), sems(9, 2), sems(3), sems(3),
            sems(NB), sems(NB), sems(ns), sems(ns), sems(nt), sems(nt),
        ],
        compiler_params=pltpu.CompilerParams(
            collective_id=0, has_side_effects=True, vmem_limit_bytes=40 * 1024 * 1024),
    )(*(pltpu.with_memory_space_constraint(x, pltpu.HBM) for x in (source, guess, field)))
    return pl.pallas_call(
        functools.partial(write_out, L),
        out_shape=[jax.ShapeDtypeStruct((L, R, C), f32)] * 3,
        in_specs=[pl.BlockSpec(memory_space=pltpu.VMEM)] * 3,
        out_specs=[pl.BlockSpec(memory_space=pltpu.HBM)] * 3,
        scratch_shapes=[sems(3, L)],
        compiler_params=pltpu.CompilerParams(vmem_limit_bytes=8 * 1024 * 1024),
    )(*outs)


def solution(mesh):
    specs = (P("tm", "slab", None),) * 3
    return jax.shard_map(on_device, mesh=mesh, in_specs=specs, out_specs=specs, check_vma=False)
```
